32 devices in a mesh: replica: 2 (over y), tp: 4 (over x, core), dp: 4 (over z).
Axes of the slice: x: 2, y: 2, z: 4, core: 2. Of those that a mesh axis runs over, the one named last changes fastest.
Arguments:
- tokens: bfloat16 [8192, 8192], P(('replica', 'dp'), 'tp'), parts along dimension 0, may hold values from -6 to 6
- query_weight: bfloat16 [8192, 4096], P(None, 'tp'), may hold values from -0.0625 to 0.0625
- value_weight: bfloat16 [8192, 1024], P(None, 'tp'), may hold values from -0.0625 to 0.0625
- adapter_down_factors: bfloat16 [256, 8192, 128], P('dp', 'tp'), may hold values from -0.0625 to 0.0625
- query_up_factors: bfloat16 [256, 64, 4096], P('dp', None, 'tp'), may hold values from -0.75 to 0.75
- value_up_factors: bfloat16 [256, 64, 1024], P('dp', None, 'tp'), may hold values from -0.75 to 0.75
- request_adapter: int32 [32], P('replica'), parts along dimension 0, may hold values from 0 to 255
- lengths: int32 [32], P('replica'), parts along dimension 0, may hold values from 1 to 1024, 4096 in all
- home: int32 [256], replicated, may hold values from 0 to 255, each once
Outputs:
- query: bfloat16 [8192, 4096], P(('replica', 'dp'), 'tp'), parts along dimension 0
- value: bfloat16 [8192, 1024], P(('replica', 'dp'), 'tp'), parts along dimension 0
The draws below stay inside these ranges and needn't reach their ends.
There are 2 independent parts, one for each index of `replica`. The reference program is written for one: setup_inputs(seed, part) draws one part's arguments, and reference() takes and returns one part's arrays. A program takes and returns all parts, laid end to end along the dimension named above; an argument that names none is the same for every part. Nothing has to cross between parts.
Inputs may be any that keep to these rules, and one draw needn't show every extreme that they name: The lengths sum to 4096; the requests lie one after another in the token order. `home`: each of 0 to 255 appears once.
All inputs are finite; a program needn't handle non-finite values.
Results may differ from the reference program's by a relative error of at most 0.0031.
Values may be sent and summed in bfloat16 or wider, within the bound.
No kernel may reach another device: no remote copies, remote signals or barrier semaphores. Data moves between devices by JAX's collectives and lax.ppermute only.
A program may use at most 192 MiB of HBM per device.

```python
import math
import jax
import jax.numpy as jnp
import numpy as np
from jax import lax

MODEL_WIDTH = 8192
QUERY_FEATURES = 4096
VALUE_FEATURES = 1024
ADAPTER_RANK = 64
ADAPTER_STORE = 256
REPLICA_REQUESTS = 16
TOKENS = 4096
LONGEST = 1024


def plant(result, key, least, top_value):
    index_at = [jax.random.randint(jax.random.fold_in(key, axis), (), 0, length) for axis, length in enumerate(result.shape)]
    longest = result.shape.index(max(result.shape))
    next_to = index_at[:longest] + [(index_at[longest] + 1) % result.shape[longest]] + index_at[longest + 1:]
    return result.at[tuple(index_at)].set(least).at[tuple(next_to)].set(top_value)


def levels(key, extent, cuts, low, largest):
    def one(axis_at, blocks):
        draws = jax.random.uniform(jax.random.fold_in(jax.random.fold_in(key, 6), axis_at), (blocks,), jnp.float32, low / len(cuts), largest / len(cuts))
        return jnp.repeat(jnp.exp(draws), extent[axis_at] // blocks).reshape((-1,) + (1,) * (len(extent) - axis_at - 1))

    level = one(*cuts[0])
    for cut in cuts[1:]:
        level = level * one(*cut)
    return level


def cumulative_ranks(amount, slope):
    weights = [(1 << 20) // math.isqrt(standing ** slope) + 1 for standing in range(1, amount + 1)]
    width = 1 + sum(weights) // (1 << 30)
    return np.cumsum(np.array([max(1, weight // width) for weight in weights]))


def ranked_ids(key, extent, number_of, lean):
    grid = cumulative_ranks(number_of, lean)
    lot = jax.random.randint(jax.random.fold_in(key, 1), extent, 0, int(grid[number_of - 1]))
    rank = jnp.searchsorted(jnp.asarray(grid, jnp.int32), lot, side="right")
    return jax.random.permutation(jax.random.fold_in(key, 2), number_of)[rank].astype(jnp.int32)


def split_up(count, total, most, lean):
    portions = [(1 << 20) // math.isqrt(rank ** lean) + 1 for rank in range(2, count + 1)]
    rest, holding = total - most - (count - 1), [1] * (count - 1)
    while rest > 0:
        candidates = [i for i in range(count - 1) if holding[i] < most]
        whole, remaining = sum([portions[i] for i in candidates]), rest
        for i in candidates:
            more = min(most - holding[i], max(1, remaining * portions[i] // whole), rest)
            holding[i] = holding[i] + more
            rest = rest - more
    return np.array([most] + holding)


def ragged(rng, number_of, total, most, slope):
    if number_of == 2:
        one = jax.random.randint(rng, (), max(1, total - most), min(most, total - 1) + 1)
        return jnp.stack([one, total - one])
    sizes = jnp.asarray(split_up(number_of, total, most, slope), jnp.int32)
    pairs = (number_of - 1) // 2
    giver, receiver = sizes[1:1 + 2 * pairs:2], sizes[2:2 + 2 * pairs:2]
    room = jnp.minimum(giver - 1, most - receiver)
    moved = jax.random.randint(jax.random.fold_in(rng, 1), (pairs,), 0, 1 << 20) % (room + 1)
    sizes = sizes.at[1:1 + 2 * pairs:2].set(giver - moved).at[2:2 + 2 * pairs:2].set(receiver + moved)
    return sizes[jax.random.permutation(jax.random.fold_in(rng, 2), number_of)]


def noise(key, dims, deviation, reach, pieces=(), held_as=jnp.bfloat16):
    result = jax.random.normal(key, dims, jnp.float32) * deviation
    if len(pieces) > 0:
        result = levels(key, dims, pieces, -0.22, 0.18) * result
    return jnp.clip(result, min=-reach, max=reach).astype(held_as)


def setup_inputs(seed: int = 0, part: int = 0) -> dict:
    arg_keys = jax.random.split(jax.random.key(seed), 10)
    part_splits = jax.random.split(jax.random.fold_in(arg_keys[9], part), 10)
    return {
        "tokens": noise(part_splits[0], (TOKENS, MODEL_WIDTH), 1.0, 6.0, ((0, 4), (1, 4))),
        "query_weight": noise(arg_keys[1], (MODEL_WIDTH, QUERY_FEATURES), MODEL_WIDTH ** -0.5, 0.0625, ((1, 4),)),
        "value_weight": noise(arg_keys[2], (MODEL_WIDTH, VALUE_FEATURES), MODEL_WIDTH ** -0.5, 0.0625, ((1, 4),)),
        "adapter_down_factors": noise(arg_keys[3], (ADAPTER_STORE, MODEL_WIDTH, 2 * ADAPTER_RANK), MODEL_WIDTH ** -0.5, 0.0625, ((0, 4), (1, 4))),
        "query_up_factors": noise(arg_keys[4], (ADAPTER_STORE, ADAPTER_RANK, QUERY_FEATURES), ADAPTER_RANK ** -0.5, 0.75, ((0, 4), (2, 4))),
        "value_up_factors": noise(arg_keys[5], (ADAPTER_STORE, ADAPTER_RANK, VALUE_FEATURES), ADAPTER_RANK ** -0.5, 0.75, ((0, 4), (2, 4))),
        "request_adapter": plant(ranked_ids(part_splits[6], (REPLICA_REQUESTS,), ADAPTER_STORE, 2), jax.random.fold_in(part_splits[6], 3), 0, ADAPTER_STORE - 1).astype(jnp.int32),
        "lengths": ragged(part_splits[7], REPLICA_REQUESTS, TOKENS, LONGEST, 2).astype(jnp.int32),
        "home": jax.random.permutation(arg_keys[8], ADAPTER_STORE).astype(jnp.int32),
    }


adapter_scale = 0.5


def reference(tokens, query_weight, value_weight, adapter_down_factors, query_up_factors, value_up_factors, request_adapter, lengths, home):
    starts = jnp.cumsum(lengths, dtype=jnp.int32) - lengths
    rows_all = jnp.arange(TOKENS, dtype=jnp.int32)
    owner = jnp.sum((rows_all[:, None] >= starts[None, :]).astype(jnp.int32), axis=1, dtype=jnp.int32) - 1
    inside = (rows_all - starts[owner]).astype(jnp.int32)
    adapter_slots = home[request_adapter]
    padded = jnp.concatenate([tokens, jnp.zeros((LONGEST, MODEL_WIDTH), tokens.dtype)], axis=0)

    def per_request(request_number):
        block_input = lax.dynamic_slice_in_dim(padded, starts[request_number].astype(jnp.int32), LONGEST, 0)
        return jnp.dot(block_input, adapter_down_factors[adapter_slots[request_number]], preferred_element_type=jnp.float32)

    blocks = lax.map(per_request, jnp.arange(REPLICA_REQUESTS, dtype=jnp.int32))
    down = blocks[owner, inside].astype(jnp.bfloat16)
    onehot = (owner[:, None] == jnp.arange(REPLICA_REQUESTS, dtype=jnp.int32)[None, :]).astype(down.dtype)
    expand_q = (onehot[:, :, None] * down[:, None, :ADAPTER_RANK]).reshape(TOKENS, REPLICA_REQUESTS * ADAPTER_RANK)
    expand_v = (onehot[:, :, None] * down[:, None, ADAPTER_RANK:]).reshape(TOKENS, REPLICA_REQUESTS * ADAPTER_RANK)
    query_stacked = query_up_factors[adapter_slots].reshape(REPLICA_REQUESTS * ADAPTER_RANK, QUERY_FEATURES)
    value_stacked = value_up_factors[adapter_slots].reshape(REPLICA_REQUESTS * ADAPTER_RANK, VALUE_FEATURES)
    query_plain = jnp.dot(tokens, query_weight, preferred_element_type=jnp.float32)
    value_plain = jnp.dot(tokens, value_weight, preferred_element_type=jnp.float32)
    query_lowrank = jnp.dot(expand_q, query_stacked, preferred_element_type=jnp.float32)
    value_lowrank = jnp.dot(expand_v, value_stacked, preferred_element_type=jnp.float32)
    query = (query_plain + adapter_scale * query_lowrank).astype(jnp.bfloat16)
    value = (value_plain + adapter_scale * value_lowrank).astype(jnp.bfloat16)
    return (query, value)
```

```python
import functools

import jax
import jax.numpy as jnp
from jax import lax
from jax.experimental import pallas as pl
from jax.experimental.pallas import tpu as pltpu
from jax.sharding import PartitionSpec as P

adapter_scale = 0.5
LAG = 2
STATIC_ROUNDS = 6
LANES = 128
ROW_TILE = 256


ANY = pl.BlockSpec(memory_space=pl.ANY)
SMEM = pl.BlockSpec(memory_space=pltpu.SMEM)
VMEM = pl.BlockSpec(memory_space=pltpu.VMEM)


def line_rounds(holder_c, far_c, first_c, holder_r, far_r, first_r, index_c, index_r, groups):
    key_c = index_c - 64.0 * far_c - 64.0 * groups * holder_c
    key_r = index_r - 64.0 * far_r - 64.0 * groups * holder_r
    rounds, crossing = [], []
    for link in range(groups - 1):
        in_c = first_c & (holder_c <= link) & (far_c > link)
        in_r = first_r & (holder_r <= link) & (far_r > link)
        place = jnp.sum(jnp.where(in_r & (key_r < key_c), 1.0, 0.0), axis=1, keepdims=True)
        place = jnp.broadcast_to(place, holder_c.shape)
        if link:
            place = jnp.where(holder_c == link, place, jnp.maximum(place, rounds[-1] + LAG))
        rounds.append(place)
        crossing.append(in_c)
    return rounds, crossing


def plan_kernel(groups, stored, rows, bound, me_ref, request_ref, lengths_ref, home_ref, out_ref):
    requests = request_ref.shape[0]
    shape = (requests, LANES)
    lane = lax.broadcasted_iota(jnp.int32, shape, 1)
    line = lax.broadcasted_iota(jnp.int32, shape, 0)
    me = me_ref[0]
    zero = jnp.zeros(shape, jnp.int32)
    slot_c, slot_r, low_c, low_r, high_c, high_r = (zero,) * 6
    begin_r, end_r = zero, zero
    start = jnp.int32(0)
    for r in range(requests):
        slot = home_ref[request_ref[r]]
        stop = start + lengths_ref[r]
        low, high = start // rows, (stop - 1) // rows
        here_c, here_r = line == r, lane == r
        slot_c, slot_r = jnp.where(here_c, slot, slot_c), jnp.where(here_r, slot, slot_r)
        low_c, low_r = jnp.where(here_c, low, low_c), jnp.where(here_r, low, low_r)
        high_c, high_r = jnp.where(here_c, high, high_c), jnp.where(here_r, high, high_r)
        begin_r = jnp.where(here_r, jnp.clip(start - me * rows, 0, rows), begin_r)
        end_r = jnp.where(here_r, jnp.clip(stop - me * rows, 0, rows), end_r)
        start = stop
    holder_c, holder_r = slot_c // stored, slot_r // stored
    place_c = (slot_c - holder_c * stored).astype(jnp.float32)
    real = lane < requests
    same = (slot_c == slot_r) & real
    f32 = lambda x: x.astype(jnp.float32)
    slot_c, slot_r, low_c, low_r, high_c, high_r, holder_c, holder_r, lane_f, line_f = (
        f32(x) for x in (slot_c, slot_r, low_c, low_r, high_c, high_r, holder_c, holder_r, lane, line)
    )
    me_f = jnp.full(shape, me, jnp.int32).astype(jnp.float32)
    wide = lambda x: jnp.broadcast_to(x, shape)
    top_c = wide(jnp.max(jnp.where(same, high_r, -1.0), axis=1, keepdims=True))
    top_r = wide(jnp.max(jnp.where(same, high_c, -1.0), axis=0, keepdims=True))
    bottom_c = wide(jnp.min(jnp.where(same, low_r, 999.0), axis=1, keepdims=True))
    bottom_r = wide(jnp.min(jnp.where(same, low_c, 999.0), axis=0, keepdims=True))
    first_c = wide(jnp.min(jnp.where(same, lane_f, 999.0), axis=1, keepdims=True)) == line_f
    first_r = wide(jnp.min(jnp.where(same, line_f, 999.0), axis=0, keepdims=True)) == lane_f
    first_r = first_r & real
    last = groups - 1.0
    streams = (
        (holder_c, top_c, holder_r, top_r, me_f),
        (last - holder_c, last - bottom_c, last - holder_r, last - bottom_r, last - me_f),
    )
    source = place_c
    most = jnp.zeros(shape, jnp.float32)
    sends = []
    for way, (hold_c, far_c, hold_r, far_r, at) in enumerate(streams):
        rounds, crossing = line_rounds(hold_c, far_c, first_c, hold_r, far_r, first_r, line_f, lane_f, groups)
        base = float(stored + way * bound)
        send = jnp.zeros(shape, jnp.float32)
        for link in range(groups - 1):
            most = jnp.maximum(most, jnp.where(crossing[link], rounds[link] + 1.0, 0.0))
            came = place_c if link == 0 else jnp.where(hold_c == link, place_c, base + rounds[link - 1])
            mine = (at == link) & crossing[link] & (rounds[link] == lane_f)
            send = send + jnp.where(mine, came, 0.0)
            source = jnp.where((at == link + 1) & (hold_c <= link), base + rounds[link], source)
        sends.append(jnp.sum(send, axis=0, keepdims=True))
    taken = jnp.sum(jnp.where(same & first_c, source, 0.0), axis=0, keepdims=True)
    most = jnp.max(jnp.max(most, axis=1, keepdims=True), axis=0, keepdims=True)
    most = jnp.broadcast_to(most, (1, LANES))
    before = jnp.sum(jnp.where((end_r[:1] == 0) & real[:1], 1.0, 0.0), axis=1, keepdims=True)
    through = jnp.sum(jnp.where((begin_r[:1] < rows) & real[:1], 1.0, 0.0), axis=1, keepdims=True)
    lane_1 = lane[:1]
    misc = jnp.where(lane_1 == 0, before, jnp.where(lane_1 == 1, through, most))
    for row, value in enumerate((*sends, taken, f32(begin_r[:1]), f32(end_r[:1]), misc)):
        out_ref[row : row + 1, :] = value.astype(jnp.int32)


def make_plan(groups, stored, rows, bound, me, request_adapter, lengths, home):
    return pl.pallas_call(
        functools.partial(plan_kernel, groups, stored, rows, bound),
        out_shape=jax.ShapeDtypeStruct((8, LANES), jnp.int32),
        in_specs=[SMEM] * 4,
        out_specs=VMEM,
        name="plan",
    )(me, request_adapter, lengths, home)


def fetch(code, stored, bound, static, local, arrived, more, start):
    @pl.when(code < stored)
    def _():
        local(code)

    for way in range(len(arrived)):
        base = stored + way * bound
        for j, ref in enumerate(arrived[way]):

            @pl.when(code == base + j)
            def _(ref=ref):
                start(ref)

        if more is not None:

            @pl.when((code >= base + static) & (code < base + bound))
            def _(way=way, base=base):
                start(more[way].at[code - base - static])


def pack_kernel(round_number, stored, bound, static, n_store, n_arrived, with_more, *refs):
    plan_ref, refs = refs[0], refs[1:]
    if with_more:
        round_number, refs = refs[0][0], refs[1:]
    store, refs = refs[:n_store], refs[n_store:]
    arrived, refs = (refs[:n_arrived], refs[n_arrived : 2 * n_arrived]), refs[2 * n_arrived :]
    more = None
    if with_more:
        more, refs = refs[:2], refs[2:]
    outs, (buf, sem) = refs[:2], refs[2:]
    for way in range(2):
        code = plan_ref[way, round_number]

        def local(place, way=way):
            at = 0
            for j, ref in enumerate(store):
                width = ref.shape[2]
                into = buf.at[way] if n_store == 1 else buf.at[way, :, pl.ds(at, width)]
                pltpu.make_async_copy(ref.at[place], into, sem.at[way]).start()
                at += width

        def start(ref, way=way):
            pltpu.make_async_copy(ref, buf.at[way], sem.at[way]).start()

        ways = tuple(a if w == way else () for w, a in enumerate(arrived))
        fetch(code, stored, bound, static, local, ways, more, start)
    for way in range(2):
        pltpu.make_async_copy(outs[way], buf.at[way], sem.at[way]).wait()
        pltpu.make_async_copy(buf.at[way], outs[way], sem.at[way]).start()
    for way in range(2):
        pltpu.make_async_copy(buf.at[way], outs[way], sem.at[way]).wait()


def pack(plan, round_number, stored, bound, static, store, arrived, more=None):
    block = (store[0].shape[1], sum(s.shape[2] for s in store))
    dtype = store[0].dtype
    operands, specs = [plan], [SMEM]
    if more is not None:
        operands, specs = operands + [round_number.reshape(1)], specs + [SMEM]
        round_number = None
    rest = [*store, *arrived[0], *arrived[1], *(more or ())]
    return pl.pallas_call(
        functools.partial(
            pack_kernel, round_number, stored, bound, static, len(store), len(arrived[0]), more is not None
        ),
        out_shape=[jax.ShapeDtypeStruct(block, dtype)] * 2,
        in_specs=specs + [ANY] * len(rest),
        out_specs=[ANY] * 2,
        scratch_shapes=[pltpu.VMEM((2, *block), dtype), pltpu.SemaphoreType.DMA((2,))],
        cost_estimate=pl.CostEstimate(flops=0, transcendentals=0, bytes_accessed=8 * block[0] * block[1]),
        name="pack",
    )(*operands, *rest)


def unset(shape, dtype):
    def kernel(out_ref):
        del out_ref

    return pl.pallas_call(kernel, out_shape=jax.ShapeDtypeStruct(shape, dtype), out_specs=ANY, name="unset")()


def down_kernel(stored, bound, static, n_arrived, plan_ref, tokens_ref, store, *refs):
    arrived, refs = (refs[:n_arrived], refs[n_arrived : 2 * n_arrived]), refs[2 * n_arrived :]
    more, (out_ref, factor, sem) = refs[:2], refs[2:]
    first, stop = plan_ref[5, 0], plan_ref[5, 1]

    def bring(r, carry):
        def start(ref):
            pltpu.make_async_copy(ref, factor.at[r], sem.at[r]).start()

        fetch(plan_ref[2, r], stored, bound, static, lambda place: start(store.at[place]), arrived, more, start)
        return carry

    lax.fori_loop(first, stop, bring, 0)
    tile = min(ROW_TILE, tokens_ref.shape[0])

    def multiply(r, carry):
        pltpu.make_async_copy(store.at[0], factor.at[r], sem.at[r]).wait()
        begin, end = plan_ref[3, r], plan_ref[4, r]

        def rows(i, carry):
            at = pl.multiple_of(i * tile, tile)
            part = jnp.dot(tokens_ref[pl.ds(at, tile), :], factor[r], preferred_element_type=jnp.float32)
            row = at + lax.broadcasted_iota(jnp.int32, part.shape, 0)
            old = out_ref[pl.ds(at, tile), :]
            out_ref[pl.ds(at, tile), :] = jnp.where((row >= begin) & (row < end), part, old)
            return carry

        return lax.fori_loop(begin // tile, (end + tile - 1) // tile, rows, carry)

    lax.fori_loop(first, stop, multiply, 0)


def down_products(plan, tokens, store, arrived, more, bound, requests):
    rows, width = tokens.shape[0], store.shape[2]
    rest = [store, *arrived[0], *arrived[1], *more]
    return pl.pallas_call(
        functools.partial(down_kernel, store.shape[0], bound, STATIC_ROUNDS, len(arrived[0])),
        out_shape=jax.ShapeDtypeStruct((rows, width), jnp.float32),
        in_specs=[SMEM, VMEM] + [ANY] * len(rest),
        out_specs=VMEM,
        scratch_shapes=[
            pltpu.VMEM((requests, *store.shape[1:]), store.dtype),
            pltpu.SemaphoreType.DMA((requests,)),
        ],
        cost_estimate=pl.CostEstimate(
            flops=4 * rows * store.shape[1] * width, transcendentals=0, bytes_accessed=4 * tokens.size
        ),
        name="down",
    )(plan, tokens, *rest)


def final_kernel(
    stored, bound, static, n_arrived, plan_ref, query_ref, value_ref, down_ref, store_q, store_v, *refs
):
    arrived, refs = (refs[:n_arrived], refs[n_arrived : 2 * n_arrived]), refs[2 * n_arrived :]
    more, refs = refs[:2], refs[2:]
    query_out, value_out, factor, total, sem = refs
    rank = store_q.shape[1]
    columns = query_ref.shape[1]
    extra = value_ref.shape[1]
    first, stop = plan_ref[5, 0], plan_ref[5, 1]
    step = pl.program_id(0)
    tile = query_ref.shape[0]

    def into(r):
        return (
            factor.at[r, pl.ds(0, rank), pl.ds(0, columns)],
            factor.at[r, pl.ds(rank, rank), pl.ds(columns, extra)],
        )

    @pl.when(step == 0)
    def _():
        def clear(r, carry):
            factor[r, :rank, columns:] = jnp.zeros((rank, extra), factor.dtype)
            factor[r, rank:, :columns] = jnp.zeros((rank, columns), factor.dtype)
            return carry

        def bring(r, carry):
            to_q, to_v = into(r)

            def local(place):
                pltpu.make_async_copy(store_q.at[place], to_q, sem.at[0, r]).start()
                pltpu.make_async_copy(store_v.at[place], to_v, sem.at[1, r]).start()

            def start(ref):
                pltpu.make_async_copy(ref.at[:, pl.ds(0, columns)], to_q, sem.at[0, r]).start()
                pltpu.make_async_copy(ref.at[:, pl.ds(columns, extra)], to_v, sem.at[1, r]).start()

            fetch(plan_ref[2, r], stored, bound, static, local, arrived, more, start)
            return carry

        def land(r, carry):
            to_q, to_v = into(r)
            pltpu.make_async_copy(store_q.at[0], to_q, sem.at[0, r]).wait()
            pltpu.make_async_copy(store_v.at[0], to_v, sem.at[1, r]).wait()
            return carry

        lax.fori_loop(first, stop, bring, 0)
        lax.fori_loop(first, stop, clear, 0)
        lax.fori_loop(first, stop, land, 0)

    total[:, :columns] = query_ref[...]
    total[:, columns:] = value_ref[...]
    at = step * tile
    scaled = down_ref[...] * jnp.asarray(adapter_scale, down_ref.dtype)
    row = at + lax.broadcasted_iota(jnp.int32, scaled.shape, 0)

    def add(r, carry):
        begin, end = plan_ref[3, r], plan_ref[4, r]

        @pl.when((begin < at + tile) & (end > at))
        def _():
            mine = jnp.where((row >= begin) & (row < end), scaled, jnp.zeros_like(scaled))
            total[...] += jnp.dot(mine, factor[r], preferred_element_type=jnp.float32)

        return carry

    lax.fori_loop(first, stop, add, 0)
    query_out[...] = total[:, :columns].astype(query_out.dtype)
    value_out[...] = total[:, columns:].astype(value_out.dtype)


def final_sum(plan, query, value, down, store_q, store_v, arrived, more, bound, requests):
    rows, columns, extra = query.shape[0], query.shape[1], value.shape[1]
    tile = min(ROW_TILE, rows)
    rest = [store_q, store_v, *arrived[0], *arrived[1], *more]
    block = lambda width: pl.BlockSpec((tile, width), lambda i: (i, 0))
    return pl.pallas_call(
        functools.partial(final_kernel, store_q.shape[0], bound, STATIC_ROUNDS, len(arrived[0])),
        grid=(rows // tile,),
        out_shape=[
            jax.ShapeDtypeStruct((rows, columns), jnp.bfloat16),
            jax.ShapeDtypeStruct((rows, extra), jnp.bfloat16),
        ],
        in_specs=[SMEM, block(columns), block(extra), block(down.shape[1])] + [ANY] * len(rest),
        out_specs=[block(columns), block(extra)],
        scratch_shapes=[
            pltpu.VMEM((requests, down.shape[1], columns + extra), store_q.dtype),
            pltpu.VMEM((tile, columns + extra), jnp.float32),
            pltpu.SemaphoreType.DMA((2, requests)),
        ],
        cost_estimate=pl.CostEstimate(
            flops=4 * rows * 256 * (columns + extra), transcendentals=0, bytes_accessed=6 * (query.size + value.size)
        ),
        name="final",
    )(plan, query, value, down, *rest)


def body(
    groups,
    shards,
    tokens,
    query_weight,
    value_weight,
    adapter_down_factors,
    query_up_factors,
    value_up_factors,
    request_adapter,
    lengths,
    home,
):
    rows, depth = tokens.shape
    stored = adapter_down_factors.shape[0]
    requests = request_adapter.shape[0]
    values = value_weight.shape[1]
    short = -values % LANES
    if short:
        value_weight = jnp.pad(value_weight, ((0, 0), (0, short)))
        value_up_factors = jnp.pad(value_up_factors, ((0, 0), (0, 0), (0, short)))
    bound = requests + LAG * groups
    me = lax.axis_index("dp")
    shard = lax.axis_index("tp")
    chips = shards // 2
    up_line = [(i, i + 1) for i in range(groups - 1)]
    down_line = [(i + 1, i) for i in range(groups - 1)]
    partner = [(i, i ^ 1) for i in range(shards)]

    def from_chip(x, away):
        return lax.ppermute(x, "tp", [(i, (i - 2 * away) % shards) for i in range(shards)])

    plan = make_plan(groups, stored, rows, bound, me.reshape(1).astype(jnp.int32), request_adapter, lengths, home)

    down_in, up_in = ([], []), ([], [])
    for stores, arrived in (((adapter_down_factors,), down_in), ((query_up_factors, value_up_factors), up_in)):
        for k in range(STATIC_ROUNDS):
            have = max(0, k - LAG + 1)
            up, low = pack(plan, k, stored, bound, STATIC_ROUNDS, stores, (arrived[0][:have], arrived[1][:have]))
            arrived[0].append(lax.ppermute(up, "dp", up_line))
            arrived[1].append(lax.ppermute(low, "dp", down_line))

    spare = bound - STATIC_ROUNDS

    def later(state):
        k, more_down, more_up = state
        out = []
        for stores, arrived, more in (
            ((adapter_down_factors,), down_in, more_down),
            ((query_up_factors, value_up_factors), up_in, more_up),
        ):
            up, low = pack(plan, k, stored, bound, STATIC_ROUNDS, stores, arrived, more)
            got = lax.ppermute(up, "dp", up_line), lax.ppermute(low, "dp", down_line)
            at = k - STATIC_ROUNDS
            out.append(tuple(lax.dynamic_update_index_in_dim(m, g, at, 0) for m, g in zip(more, got)))
        return k + 1, *out

    down_block = adapter_down_factors.shape[1:]
    up_block = (query_up_factors.shape[1], query_up_factors.shape[2] + value_up_factors.shape[2])
    dtype = tokens.dtype
    state = (
        jnp.int32(STATIC_ROUNDS),
        tuple(unset((spare, *down_block), dtype) for _ in range(2)),
        tuple(unset((spare, *up_block), dtype) for _ in range(2)),
    )
    _, more_down, more_up = lax.while_loop(lambda s: s[0] < plan[5, 2], later, state)

    share = down_products(plan, tokens, adapter_down_factors, down_in, more_down, bound, requests)
    share = share + lax.ppermute(share, "tp", partner)
    down = share
    for away in range(1, chips):
        down = down + from_chip(share, away)
    down = down.astype(jnp.bfloat16)

    def product(x, which):
        at = (which * depth, jnp.zeros((), which.dtype))
        q = lax.dynamic_slice(query_weight, at, (depth, query_weight.shape[1]))
        v = lax.dynamic_slice(value_weight, at, (depth, value_weight.shape[1]))
        dot = functools.partial(jnp.dot, preferred_element_type=jnp.float32)
        return dot(x, q), dot(x, v)

    def plus(a, b):
        return a[0] + b[0], a[1] + b[1]

    total = plus(product(tokens, shard), product(lax.ppermute(tokens, "tp", partner), shard ^ 1))
    pieces = 4
    size = rows // pieces
    parts = []
    for p in range(pieces):
        part = tuple(t[p * size : (p + 1) * size] for t in total)
        for away in range(1, chips):
            mine = from_chip(tokens[p * size : (p + 1) * size], away)
            other = lax.ppermute(mine, "tp", partner)
            which = (shard + 2 * away) % shards
            part = plus(part, plus(product(mine, which), product(other, which ^ 1)))
        parts.append(part)
    query = jnp.concatenate([p[0] for p in parts])
    value = jnp.concatenate([p[1] for p in parts])
    query, value = final_sum(
        plan, query, value, down, query_up_factors, value_up_factors, up_in, more_up, bound, requests
    )
    return (query, value[:, :values] if short else value)


def solution(mesh):
    in_specs = (
        P(("replica", "dp"), "tp"),
        P(None, "tp"),
        P(None, "tp"),
        P("dp", "tp", None),
        P("dp", None, "tp"),
        P("dp", None, "tp"),
        P("replica"),
        P("replica"),
        P(),
    )
    out_specs = (P(("replica", "dp"), "tp"), P(("replica", "dp"), "tp"))
    step = functools.partial(body, mesh.shape["dp"], mesh.shape["tp"])
    return jax.shard_map(step, mesh=mesh, in_specs=in_specs, out_specs=out_specs, check_vma=False)
```

```python
import functools
import itertools
import math

import jax
import jax.numpy as jnp
from jax import lax
from jax.experimental import pallas as pl
from jax.experimental.pallas import tpu as pltpu
from jax.sharding import PartitionSpec as P

adapter_scale = 0.5
LAG = 2
DOWN_ROUNDS = (1, 1, 1, 1, 1, 1, 1)
UP_ROUNDS = (2, 2, 2, 1)
LANES = 128
ROW_TILE = 256
COLUMN_TILE = 256
PIECES = 4


ANY = pl.BlockSpec(memory_space=pl.ANY)
SMEM = pl.BlockSpec(memory_space=pltpu.SMEM)
VMEM = pl.BlockSpec(memory_space=pltpu.VMEM)


def line_rounds(holder_c, far_c, first_c, holder_r, far_r, first_r, index_c, index_r, groups):
    key_c = index_c - 64.0 * far_c - 64.0 * groups * holder_c
    key_r = index_r - 64.0 * far_r - 64.0 * groups * holder_r
    rounds, crossing = [], []
    for link in range(groups - 1):
        in_c = first_c & (holder_c <= link) & (far_c > link)
        in_r = first_r & (holder_r <= link) & (far_r > link)
        place = jnp.sum(jnp.where(in_r & (key_r < key_c), 1.0, 0.0), axis=1, keepdims=True)
        place = jnp.broadcast_to(place, holder_c.shape)
        if link:
            place = jnp.where(holder_c == link, place, jnp.maximum(place, rounds[-1] + LAG))
        rounds.append(place)
        crossing.append(in_c)
    return rounds, crossing


def plan_kernel(groups, stored, rows, bound, me_ref, request_ref, lengths_ref, home_ref, out_ref):
    requests = request_ref.shape[0]
    shape = (requests, LANES)
    lane = lax.broadcasted_iota(jnp.int32, shape, 1)
    line = lax.broadcasted_iota(jnp.int32, shape, 0)
    me = me_ref[0]
    zero = jnp.zeros(shape, jnp.int32)
    slot_c, slot_r, low_c, low_r, high_c, high_r = (zero,) * 6
    begin_r, end_r = zero, zero
    start = jnp.int32(0)
    for r in range(requests):
        slot = home_ref[request_ref[r]]
        stop = start + lengths_ref[r]
        low, high = start // rows, (stop - 1) // rows
        here_c, here_r = line == r, lane == r
        slot_c, slot_r = jnp.where(here_c, slot, slot_c), jnp.where(here_r, slot, slot_r)
        low_c, low_r = jnp.where(here_c, low, low_c), jnp.where(here_r, low, low_r)
        high_c, high_r = jnp.where(here_c, high, high_c), jnp.where(here_r, high, high_r)
        begin_r = jnp.where(here_r, jnp.clip(start - me * rows, 0, rows), begin_r)
        end_r = jnp.where(here_r, jnp.clip(stop - me * rows, 0, rows), end_r)
        start = stop
    holder_c, holder_r = slot_c // stored, slot_r // stored
    place_c = (slot_c - holder_c * stored).astype(jnp.float32)
    real = lane < requests
    same = (slot_c == slot_r) & real
    f32 = lambda x: x.astype(jnp.float32)
    slot_c, slot_r, low_c, low_r, high_c, high_r, holder_c, holder_r, lane_f, line_f = (
        f32(x) for x in (slot_c, slot_r, low_c, low_r, high_c, high_r, holder_c, holder_r, lane, line)
    )
    me_f = jnp.full(shape, me, jnp.int32).astype(jnp.float32)
    wide = lambda x: jnp.broadcast_to(x, shape)
    top_c = wide(jnp.max(jnp.where(same, high_r, -1.0), axis=1, keepdims=True))
    top_r = wide(jnp.max(jnp.where(same, high_c, -1.0), axis=0, keepdims=True))
    bottom_c = wide(jnp.min(jnp.where(same, low_r, 999.0), axis=1, keepdims=True))
    bottom_r = wide(jnp.min(jnp.where(same, low_c, 999.0), axis=0, keepdims=True))
    first_c = wide(jnp.min(jnp.where(same, lane_f, 999.0), axis=1, keepdims=True)) == line_f
    first_r = wide(jnp.min(jnp.where(same, line_f, 999.0), axis=0, keepdims=True)) == lane_f
    first_r = first_r & real
    last = groups - 1.0
    streams = (
        (holder_c, top_c, holder_r, top_r, me_f),
        (last - holder_c, last - bottom_c, last - holder_r, last - bottom_r, last - me_f),
    )
    odd = lax.rem(me, 2)
    odd_f = jnp.full(shape, odd, jnp.int32).astype(jnp.float32)
    source = place_c
    most = jnp.zeros(shape, jnp.float32)
    sends = []
    for way, (hold_c, far_c, hold_r, far_r, at) in enumerate(streams):
        rounds, crossing = line_rounds(hold_c, far_c, first_c, hold_r, far_r, first_r, line_f, lane_f, groups)
        base = stored + bound * (odd_f if way else 1.0 - odd_f)
        send = jnp.zeros(shape, jnp.float32)
        for link in range(groups - 1):
            most = jnp.maximum(most, jnp.where(crossing[link], rounds[link] + 1.0, 0.0))
            came = place_c if link == 0 else jnp.where(hold_c == link, place_c, base + rounds[link - 1])
            mine = (at == link) & crossing[link] & (rounds[link] == lane_f)
            send = send + jnp.where(mine, came, 0.0)
            source = jnp.where((at == link + 1) & (hold_c <= link), base + rounds[link], source)
        sends.append(jnp.sum(send, axis=0, keepdims=True))
    taken = jnp.sum(jnp.where(same & first_c, source, 0.0), axis=0, keepdims=True)
    most = jnp.max(jnp.max(most, axis=1, keepdims=True), axis=0, keepdims=True)
    most = jnp.broadcast_to(most, (1, LANES))
    before = jnp.sum(jnp.where((end_r[:1] == 0) & real[:1], 1.0, 0.0), axis=1, keepdims=True)
    through = jnp.sum(jnp.where((begin_r[:1] < rows) & real[:1], 1.0, 0.0), axis=1, keepdims=True)
    lane_1 = lane[:1]
    misc = jnp.where(lane_1 == 0, before, jnp.where(lane_1 == 1, through, most))
    swap = odd_f[:1] > 0.5
    sends = jnp.where(swap, sends[1], sends[0]), jnp.where(swap, sends[0], sends[1])
    for row, value in enumerate((*sends, taken, f32(begin_r[:1]), f32(end_r[:1]), misc)):
        out_ref[row : row + 1, :] = value.astype(jnp.int32)


def make_plan(groups, stored, rows, bound, me, request_adapter, lengths, home):
    return pl.pallas_call(
        functools.partial(plan_kernel, groups, stored, rows, bound),
        out_shape=jax.ShapeDtypeStruct((8, LANES), jnp.int32),
        in_specs=[SMEM] * 4,
        out_specs=VMEM,
        name="plan",
    )(me, request_adapter, lengths, home)


def fetch(code, stored, bound, static, local, arrived, more, start):
    if more is None:
        for way in range(len(arrived)):
            base = stored + way * bound
            code = jnp.where((code >= base + static) & (code < base + bound), 0, code)

    @pl.when(code < stored)
    def _():
        local(code)

    for way in range(len(arrived)):
        base = stored + way * bound
        for j, ref in enumerate(arrived[way]):

            @pl.when(code == base + j)
            def _(ref=ref):
                start(ref)

        if more is not None:

            @pl.when((code >= base + static) & (code < base + bound))
            def _(way=way, base=base):
                start(more[way].at[code - base - static])


def single(refs):
    return [ref.at[j] for ref in refs for j in range(ref.shape[0])]


def pack_kernel(rounds, stored, bound, static, n_store, n_arrived, with_more, *refs):
    plan_ref, refs = refs[0], refs[1:]
    if with_more:
        rounds, refs = ((refs[0][0],),), refs[1:]
    store, refs = refs[:n_store], refs[n_store:]
    arrived, refs = (single(refs[:n_arrived]), single(refs[n_arrived : 2 * n_arrived])), refs[2 * n_arrived :]
    more = None
    if with_more:
        more, refs = refs[:2], refs[2:]
    outs, (buf, sem) = refs[: 2 * len(rounds)], refs[2 * len(rounds) :]
    blocks = []
    for m, message in enumerate(rounds):
        for way in range(2):
            for j, number in enumerate(message):
                blocks.append((way, number, outs[2 * m + way].at[j]))
    for n, (way, number, _) in enumerate(blocks):

        def local(place, n=n):
            at = 0
            for ref in store:
                width = ref.shape[2]
                into = buf.at[n] if n_store == 1 else buf.at[n, :, pl.ds(at, width)]
                pltpu.make_async_copy(ref.at[place], into, sem.at[n]).start()
                at += width

        def start(ref, n=n):
            pltpu.make_async_copy(ref, buf.at[n], sem.at[n]).start()

        ways = tuple(a if w != way else () for w, a in enumerate(arrived))
        fetch(plan_ref[way, number], stored, bound, static, local, ways, more, start)
    for n, (_, _, out) in enumerate(blocks):
        pltpu.make_async_copy(out, buf.at[n], sem.at[n]).wait()
        pltpu.make_async_copy(buf.at[n], out, sem.at[n]).start()
    for n, (_, _, out) in enumerate(blocks):
        pltpu.make_async_copy(buf.at[n], out, sem.at[n]).wait()


def pack(plan, rounds, stored, bound, static, store, arrived, more=None):
    block = (store[0].shape[1], sum(s.shape[2] for s in store))
    dtype = store[0].dtype
    operands, specs = [plan], [SMEM]
    if more is not None:
        operands, specs = operands + [rounds.reshape(1)], specs + [SMEM]
        rounds = ((None,),)
    n_blocks = 2 * sum(len(m) for m in rounds)
    rest = [*store, *arrived[0], *arrived[1], *(more or ())]
    return pl.pallas_call(
        functools.partial(pack_kernel, rounds, stored, bound, static, len(store), len(arrived[0]), more is not None),
        out_shape=[jax.ShapeDtypeStruct((len(m), *block), dtype) for m in rounds for _ in range(2)],
        in_specs=specs + [ANY] * len(rest),
        out_specs=[ANY] * (2 * len(rounds)),
        scratch_shapes=[pltpu.VMEM((n_blocks, *block), dtype), pltpu.SemaphoreType.DMA((n_blocks,))],
        cost_estimate=pl.CostEstimate(
            flops=0, transcendentals=0, bytes_accessed=4 * n_blocks * block[0] * block[1]
        ),
        name="pack",
    )(*operands, *rest)


def unset(shape, dtype):
    def kernel(out_ref):
        del out_ref

    return pl.pallas_call(kernel, out_shape=jax.ShapeDtypeStruct(shape, dtype), out_specs=ANY, name="unset")()


def down_kernel(stored, bound, static, n_arrived, plan_ref, tokens_ref, store, *refs):
    arrived, refs = (single(refs[:n_arrived]), single(refs[n_arrived : 2 * n_arrived])), refs[2 * n_arrived :]
    more, (out_ref, factor, sem) = refs[:-3] or None, refs[-3:]
    first, stop = plan_ref[5, 0], plan_ref[5, 1]

    def bring(r, carry):
        def start(ref):
            pltpu.make_async_copy(ref, factor.at[r], sem.at[r]).start()

        fetch(plan_ref[2, r], stored, bound, static, lambda place: start(store.at[place]), arrived, more, start)
        return carry

    lax.fori_loop(first, stop, bring, 0)
    tile = min(ROW_TILE, tokens_ref.shape[0])

    def multiply(r, carry):
        pltpu.make_async_copy(store.at[0], factor.at[r], sem.at[r]).wait()
        begin, end = plan_ref[3, r], plan_ref[4, r]

        def rows(i, carry):
            at = pl.multiple_of(i * tile, tile)
            part = jnp.dot(tokens_ref[pl.ds(at, tile), :], factor[r], preferred_element_type=jnp.float32)
            row = at + lax.broadcasted_iota(jnp.int32, part.shape, 0)
            old = out_ref[pl.ds(at, tile), :]
            out_ref[pl.ds(at, tile), :] = jnp.where((row >= begin) & (row < end), part, old)
            return carry

        return lax.fori_loop(begin // tile, (end + tile - 1) // tile, rows, carry)

    lax.fori_loop(first, stop, multiply, 0)


def down_products(plan, tokens, store, arrived, more, bound, requests):
    rows, width = tokens.shape[0], store.shape[2]
    rest = [store, *arrived[0], *arrived[1], *more]
    return pl.pallas_call(
        functools.partial(down_kernel, store.shape[0], bound, sum(DOWN_ROUNDS), len(arrived[0])),
        out_shape=jax.ShapeDtypeStruct((rows, width), jnp.float32),
        in_specs=[SMEM, VMEM] + [ANY] * len(rest),
        out_specs=VMEM,
        scratch_shapes=[
            pltpu.VMEM((requests, *store.shape[1:]), store.dtype),
            pltpu.SemaphoreType.DMA((requests,)),
        ],
        cost_estimate=pl.CostEstimate(
            flops=4 * rows * store.shape[1] * width, transcendentals=0, bytes_accessed=4 * tokens.size
        ),
        name="down",
    )(plan, tokens, *rest)


def product_tile(lhs, tiles):
    return sum(jnp.dot(x[...], w[...], preferred_element_type=jnp.float32) for x, w in zip(lhs, tiles))


def product_kernel(query_steps, with_sum, n, which_ref, *refs):
    lhs, queries, values, refs = refs[:n], refs[n : 2 * n], refs[2 * n : 3 * n], refs[3 * n :]
    out_ref = refs[-1]
    for on, tiles in ((pl.program_id(0) < query_steps, queries), (pl.program_id(0) >= query_steps, values)):

        @pl.when(on)
        def _(tiles=tiles):
            part = product_tile(lhs, tiles)
            out_ref[...] = part + refs[0][...] if with_sum else part


def product_specs(n, rows, depth, columns, tile, piece, pieces):
    steps = columns // tile
    full = pl.BlockSpec((rows, depth), lambda g, *_: (0, 0))

    def of_query(j):
        return pl.BlockSpec((depth, tile), lambda g, w, *_: (w[j] * pieces + piece, jnp.minimum(g, steps - 1)))

    def of_value(j):
        return pl.BlockSpec((depth, tile), lambda g, w, *_: (w[j] * pieces + piece, jnp.maximum(g - steps, 0)))

    return [full] * n + [of_query(j) for j in range(n)] + [of_value(j) for j in range(n)]


def product(which, lhs, piece, pieces, query_weight, value_weight, total=None):
    rows, depth = lhs[0].shape
    n = len(lhs)
    columns, extra = query_weight.shape[1], value_weight.shape[1]
    tile = math.gcd(columns, extra, COLUMN_TILE)
    specs = product_specs(n, rows, depth, columns, tile, piece, pieces)
    operands = [*lhs, *[query_weight] * n, *[value_weight] * n]
    block = pl.BlockSpec((rows, tile), lambda g, w: (0, g))
    if total is not None:
        specs, operands = specs + [block], operands + [total]
    return pl.pallas_call(
        functools.partial(product_kernel, columns // tile, total is not None, n),
        grid_spec=pltpu.PrefetchScalarGridSpec(
            num_scalar_prefetch=1, grid=((columns + extra) // tile,), in_specs=specs, out_specs=block
        ),
        out_shape=jax.ShapeDtypeStruct((rows, columns + extra), jnp.float32),
        cost_estimate=pl.CostEstimate(
            flops=2 * n * rows * depth * (columns + extra), transcendentals=0, bytes_accessed=8 * rows * (columns + extra)
        ),
        name="product",
    )(which, *operands)


def final_kernel(stored, bound, static, n_arrived, which_ref, plan_ref, *refs):
    lhs, refs = refs[:2], refs[2:]
    queries, values, refs = refs[:2], refs[2:4], refs[4:]
    total_ref, down_ref, store_q, store_v = refs[:4]
    refs = refs[4:]
    arrived, refs = (single(refs[:n_arrived]), single(refs[n_arrived : 2 * n_arrived])), refs[2 * n_arrived :]
    more, refs = refs[:2], refs[2:]
    query_out, value_out, factor, spread, sem = refs
    rank, columns, extra = store_q.shape[1], store_q.shape[2], store_v.shape[2]
    width = down_ref.shape[1]
    first, stop = plan_ref[5, 0], plan_ref[5, 1]
    first_pair, stop_pair = first // 2, (stop + 1) // 2
    step = pl.program_id(0)
    tile = total_ref.shape[1]
    steps = columns // tile

    @pl.when(step == 0)
    def _():
        def into(r):
            at = pl.multiple_of(lax.rem(r, 2) * width, width)
            return (
                factor.at[r // 2, pl.ds(at, rank), pl.ds(0, columns)],
                factor.at[r // 2, pl.ds(at + rank, rank), pl.ds(columns, extra)],
            )

        def bring(r, carry):
            to_q, to_v = into(r)

            def local(place):
                pltpu.make_async_copy(store_q.at[place], to_q, sem.at[0, r]).start()
                pltpu.make_async_copy(store_v.at[place], to_v, sem.at[1, r]).start()

            def start(ref):
                pltpu.make_async_copy(ref.at[:, pl.ds(0, columns)], to_q, sem.at[0, r]).start()
                pltpu.make_async_copy(ref.at[:, pl.ds(columns, extra)], to_v, sem.at[1, r]).start()

            fetch(plan_ref[2, r], stored, bound, static, local, arrived, more, start)
            return carry

        def land(r, carry):
            to_q, to_v = into(r)
            pltpu.make_async_copy(store_q.at[0], to_q, sem.at[0, r]).wait()
            pltpu.make_async_copy(store_v.at[0], to_v, sem.at[1, r]).wait()
            return carry

        scaled = down_ref[...] * jnp.asarray(adapter_scale, down_ref.dtype)
        row = lax.broadcasted_iota(jnp.int32, scaled.shape, 0)

        def prepare(p, carry):
            for half in range(2):
                r, at = 2 * p + half, half * width
                used = (r >= first) & (r < stop)
                factor[p, at : at + rank, columns:] = jnp.zeros((rank, extra), factor.dtype)
                factor[p, at + rank : at + width, :columns] = jnp.zeros((width - rank, columns), factor.dtype)

                @pl.when(jnp.logical_not(used))
                def _(at=at):
                    factor[p, at : at + rank, :columns] = jnp.zeros((rank, columns), factor.dtype)
                    factor[p, at + rank : at + width, columns:] = jnp.zeros((width - rank, extra), factor.dtype)

                mine = used & (row >= plan_ref[3, r]) & (row < plan_ref[4, r])
                spread[p, :, at : at + width] = jnp.where(mine, scaled, jnp.zeros_like(scaled))
            return carry

        lax.fori_loop(first, stop, bring, 0)
        lax.fori_loop(first_pair, stop_pair, prepare, 0)
        lax.fori_loop(first, stop, land, 0)

    def emit(out_ref, tiles):
        def add(p, total):
            at = pl.multiple_of(step * tile, tile)
            return total + jnp.dot(spread[p], factor[p, :, pl.ds(at, tile)], preferred_element_type=jnp.float32)

        total = total_ref[...] + product_tile(lhs, tiles)
        out_ref[...] = lax.fori_loop(first_pair, stop_pair, add, total).astype(out_ref.dtype)

    @pl.when(step < steps)
    def _():
        emit(query_out, queries)

    @pl.when(step >= steps)
    def _():
        emit(value_out, values)


def final(
    which, plan, lhs, piece, pieces, query_weight, value_weight, total, down, store_q, store_v, arrived, more, bound,
    requests,
):
    rows, depth = lhs[0].shape
    columns, extra = query_weight.shape[1], value_weight.shape[1]
    tile = math.gcd(columns, extra, COLUMN_TILE)
    steps = columns // tile
    rest = [store_q, store_v, *arrived[0], *arrived[1], *more]
    width = down.shape[1]
    return pl.pallas_call(
        functools.partial(final_kernel, store_q.shape[0], bound, sum(UP_ROUNDS), len(arrived[0])),
        grid_spec=pltpu.PrefetchScalarGridSpec(
            num_scalar_prefetch=2,
            grid=((columns + extra) // tile,),
            in_specs=[
                *product_specs(2, rows, depth, columns, tile, piece, pieces),
                pl.BlockSpec((rows, tile), lambda g, *_: (0, g)),
                pl.BlockSpec((rows, width), lambda g, *_: (0, 0)),
                *([ANY] * len(rest)),
            ],
            out_specs=[
                pl.BlockSpec((rows, tile), lambda g, *_: (0, jnp.minimum(g, steps - 1))),
                pl.BlockSpec((rows, tile), lambda g, *_: (0, jnp.maximum(g - steps, 0))),
            ],
            scratch_shapes=[
                pltpu.VMEM((pl.cdiv(requests, 2), 2 * width, columns + extra), store_q.dtype),
                pltpu.VMEM((pl.cdiv(requests, 2), rows, 2 * width), down.dtype),
                pltpu.SemaphoreType.DMA((2, requests)),
            ],
        ),
        out_shape=[
            jax.ShapeDtypeStruct((rows, columns), jnp.bfloat16),
            jax.ShapeDtypeStruct((rows, extra), jnp.bfloat16),
        ],
        cost_estimate=pl.CostEstimate(
            flops=4 * rows * (depth + 512) * (columns + extra),
            transcendentals=0,
            bytes_accessed=6 * rows * (columns + extra),
        ),
        name="final",
    )(which, plan, *lhs, query_weight, query_weight, value_weight, value_weight, total, down, *rest)


def body(
    replicas,
    groups,
    shards,
    tokens,
    query_weight,
    value_weight,
    adapter_down_factors,
    query_up_factors,
    value_up_factors,
    request_adapter,
    lengths,
    home,
):
    rows, depth = tokens.shape
    stored = adapter_down_factors.shape[0]
    requests = request_adapter.shape[0]
    values = value_weight.shape[1]
    short = -values % LANES
    if short:
        value_weight = jnp.pad(value_weight, ((0, 0), (0, short)))
        value_up_factors = jnp.pad(value_up_factors, ((0, 0), (0, 0), (0, short)))
    bound = requests + LAG * groups
    me = lax.axis_index("dp")
    shard = lax.axis_index("tp")
    chips = shards // 2
    partner = [(i, i ^ 1) for i in range(shards)]
    swap = [i ^ 1 if i ^ 1 < groups else i for i in range(groups)], [
        j if 0 <= (j := ((i + 1) ^ 1) - 1) < groups else i for i in range(groups)
    ]

    def from_chip(x, away):
        return lax.ppermute(x, "tp", [(i, (i - 2 * away) % shards) for i in range(shards)])

    def hop(messages):
        out = []
        for way, m in enumerate(messages):
            out.append(lax.ppermute(m, "dp", list(enumerate(swap[way]))))
        return out

    depth_piece = depth // PIECES
    own = [tokens[:, p * depth_piece : (p + 1) * depth_piece] for p in range(PIECES)]
    plan = make_plan(groups, stored, rows, bound, me.reshape(1).astype(jnp.int32), request_adapter, lengths, home)
    remote = []
    for away in range(1, chips):
        for p in range(PIECES):
            remote.append((away, p, from_chip(own[p], away)))
    neighbour = lax.ppermute(tokens, "tp", partner)

    most = plan[5, 2]
    for away in range(1, replicas):
        turn = [(i, (i + away) % replicas) for i in range(replicas)]
        most = jnp.maximum(most, lax.ppermute(plan, "replica", turn)[5, 2])

    def travel(stores, counts):
        arrived = [], []
        ends = list(itertools.accumulate(counts))
        for count, end in zip(counts, ends):
            numbers = tuple(range(end - count, end))
            have = sum(e - c <= end - 1 - LAG for c, e in zip(counts, ends))
            got = pack(plan, (numbers,), stored, bound, ends[-1], stores, (arrived[0][:have], arrived[1][:have]))
            got = hop(got)
            for way in range(2):
                arrived[way].append(got[way])
        return arrived

    down_stores, up_stores = (adapter_down_factors,), (query_up_factors, value_up_factors)
    down_in = travel(down_stores, DOWN_ROUNDS)
    up_in = travel(up_stores, UP_ROUNDS)

    def down_sum(plan, tokens, arrived, more):
        share = down_products(plan, tokens, adapter_down_factors, arrived, more, bound, requests)
        share = share + lax.ppermute(share, "tp", partner)
        down, sent = share, share.astype(jnp.bfloat16)
        for away in range(1, chips):
            down = down + from_chip(sent, away).astype(jnp.float32)
        return down.astype(jnp.bfloat16)

    down = down_sum(plan, tokens, down_in, ())

    weights = query_weight, value_weight
    total = product(shard.reshape(1), (tokens,), 0, 1, *weights)
    total = product((shard ^ 1).reshape(1), (neighbour,), 0, 1, *weights, total)
    for away, p, mine in remote:
        other = lax.ppermute(mine, "tp", partner)
        which = (shard + 2 * away) % shards
        which = jnp.stack([which, which ^ 1])
        if (away, p) != remote[-1][:2]:
            total = product(which, (mine, other), p, PIECES, *weights, total)
    held = plan, most, down, down_in, up_in, mine, other
    plan, most, down, down_in, up_in, mine, other = lax.optimization_barrier(held)
    odd = lax.rem(me, 2) == 1
    up_line = [(i, i + 1) for i in range(groups - 1)]
    low_line = [(i + 1, i) for i in range(groups - 1)]
    kinds = (down_stores, DOWN_ROUNDS), (up_stores, UP_ROUNDS)

    def blank():
        return tuple(
            tuple(
                unset((bound - sum(c), s[0].shape[1], sum(x.shape[2] for x in s)), tokens.dtype) for _ in range(2)
            )
            for s, c in kinds
        )

    def late(plan, most, down, down_in, up_in):
        def step(state):
            k, all_more = state
            new = []
            for (stores, counts), arrived, more in zip(kinds, (down_in, up_in), all_more):
                fixed = sum(counts)
                sent = pack(plan, k, stored, bound, fixed, stores, arrived, more)
                got = (
                    lax.ppermute(jnp.where(odd, sent[1], sent[0]), "dp", up_line),
                    lax.ppermute(jnp.where(odd, sent[0], sent[1]), "dp", low_line),
                )
                got = jnp.where(odd, got[0], got[1]), jnp.where(odd, got[1], got[0])
                new.append(tuple(lax.dynamic_update_slice_in_dim(m, g, k - fixed, 0) for m, g in zip(more, got)))
            return k + 1, tuple(new)

        start = jnp.int32(sum(DOWN_ROUNDS)), blank()
        _, (down_more, up_more) = lax.while_loop(lambda s: s[0] < most, step, start)
        return down_sum(plan, tokens, down_in, down_more), up_more

    down, up_more = lax.cond(
        most > sum(DOWN_ROUNDS), late, lambda p, m, d, *_: (d, blank()[1]), plan, most, down, down_in, up_in
    )
    query, value = final(
        which, plan, (mine, other), p, PIECES, *weights, total, down, query_up_factors, value_up_factors, up_in,
        up_more, bound, requests,
    )
    return (query, value[:, :values] if short else value)


def solution(mesh):
    in_specs = (
        P(("replica", "dp"), "tp"),
        P(None, "tp"),
        P(None, "tp"),
        P("dp", "tp", None),
        P("dp", None, "tp"),
        P("dp", None, "tp"),
        P("replica"),
        P("replica"),
        P(),
    )
    out_specs = (P(("replica", "dp"), "tp"), P(("replica", "dp"), "tp"))
    step = functools.partial(body, mesh.shape["replica"], mesh.shape["dp"], mesh.shape["tp"])
    step = jax.shard_map(step, mesh=mesh, in_specs=in_specs, out_specs=out_specs, check_vma=False)
    return step
```
